128 devices in a mesh: ctx: 64 (over z, x, y), head: 2 (over core).
Axes of the slice: x: 4, y: 4, z: 4, core: 2. Of those that a mesh axis runs over, the one named last changes fastest.
Arguments:
- queries: bfloat16 [16384, 2048], P('ctx', 'head'), may hold values from -6 to 6
- keys: bfloat16 [16384, 2048], P('ctx', 'head'), may hold values from -6 to 6
- values: bfloat16 [16384, 2048], P('ctx', 'head'), may hold values from -6 to 6
- out_weight: bfloat16 [2048, 2048], P('head'), may hold values from -0.125 to 0.125
- grad_out: bfloat16 [16384, 2048], P('ctx', 'head'), may hold values from -16 to 16
- doc_ids: int32 [16384], P('ctx'), may hold values from 0 to 3, never falling along the last dimension, each value on 1 to 8192 neighbouring positions
Outputs:
- grad_queries: bfloat16 [16384, 2048], P('ctx', 'head')
- grad_keys: bfloat16 [16384, 2048], P('ctx', 'head')
- grad_values: bfloat16 [16384, 2048], P('ctx', 'head')
- grad_weight: float32 [2048, 16, 128], P('ctx', 'head')
The draws below stay inside these ranges and needn't reach their ends.
Inputs may be any that keep to these rules, and one draw needn't show every extreme that they name: `doc_ids`: document numbers never fall along the sequence and start at 0; all 4 documents occur, each 1 to 8192 positions long, one exactly 8192.
All inputs are finite; a program needn't handle non-finite values.
Results may differ from the reference program's by a relative error of at most 0.018.
Values may be sent and summed in bfloat16 or wider, within the bound.
A program may use at most 192 MiB of HBM per device.

```python
import math
import jax
import jax.numpy as jnp
import numpy as np
from jax import lax

H = 16
HD = 128
D = 2048
DOCS = 4
SEQ = 16384


def with_spikes(drawn, rng, source, target, shards_of, factor):
    owner, partner = [(jnp.arange(drawn.shape[dim]) // (drawn.shape[dim] // shards_of)).reshape([-1 if axis == dim else 1 for axis in range(drawn.ndim)]) for dim in (source, target)]
    chosen = jax.random.permutation(rng, shards_of)[partner]
    strong = (owner == chosen) | (owner == (partner + shards_of // 2) % shards_of)
    return jnp.where(strong, factor * drawn, drawn)


def shard_levels(stream_key, shape, cuts, low, top_value):
    loudness, own = 1.0, jax.random.fold_in(stream_key, 6)
    for axis_at, parts in cuts:
        heights = jnp.exp(jax.random.uniform(jax.random.fold_in(own, axis_at), (parts,), jnp.float32, low / len(cuts), top_value / len(cuts)))
        loudness = loudness * jnp.repeat(heights, shape[axis_at] // parts).reshape([-1 if axis == axis_at else 1 for axis in range(len(shape))])
    return loudness


def length_profile(number_of, total, bound, lean):
    weights = [(1 << 20) // math.isqrt(rank ** lean) + 1 for rank in range(2, number_of + 1)]
    rest, given = total - bound - (number_of - 1), [1] * (number_of - 1)
    while rest > 0:
        movable = [i for i in range(number_of - 1) if given[i] < bound]
        pool, budget = sum([weights[i] for i in movable]), rest
        for i in movable:
            more = min(bound - given[i], max(1, budget * weights[i] // pool), rest)
            given[i] = given[i] + more
            rest = rest - more
    return np.array([bound] + given)


def ragged(rng, count, total, reach, slope):
    if count == 2:
        one = jax.random.randint(rng, (), max(1, total - reach), min(reach, total - 1) + 1)
        return jnp.stack([one, total - one])
    sizes = jnp.asarray(length_profile(count, total, reach, slope), jnp.int32)
    pairs = (count - 1) // 2
    donor, taker = sizes[1:1 + 2 * pairs:2], sizes[2:2 + 2 * pairs:2]
    slack = jnp.minimum(donor - 1, reach - taker)
    passed = jax.random.randint(jax.random.fold_in(rng, 1), (pairs,), 0, 1 << 20) % (slack + 1)
    sizes = sizes.at[1:1 + 2 * pairs:2].set(donor - passed).at[2:2 + 2 * pairs:2].set(taker + passed)
    return sizes[jax.random.permutation(jax.random.fold_in(rng, 2), count)]


def centred(stream_key, extent, deviation, limit, cuts=(), dtype=jnp.bfloat16):
    gain = shard_levels(stream_key, extent, cuts, -0.22, 0.18) if cuts else 1.0
    values = jax.random.normal(stream_key, extent, jnp.float32) * deviation * gain
    return jnp.minimum(jnp.maximum(values, -limit), limit).astype(dtype)


def noise_with(own_key, shape, deviation, reach, cuts, heavy, dtype=jnp.bfloat16):
    drawn = deviation * jax.random.normal(own_key, shape, jnp.float32)
    if cuts:
        drawn = drawn * shard_levels(own_key, shape, cuts, -0.22, 0.18)
    return jnp.clip(with_spikes(drawn, jax.random.fold_in(own_key, 3), *heavy), -reach, reach).astype(dtype)


def setup_inputs(seed: int = 0) -> dict:
    arg_keys = jax.random.split(jax.random.key(seed), 7)
    return {
        "queries": centred(arg_keys[0], (SEQ, D), 1.0, 6.0, ((0, 64), (1, 2))),
        "keys": centred(arg_keys[1], (SEQ, D), 1.0, 6.0, ((0, 64), (1, 2))),
        "values": centred(arg_keys[2], (SEQ, D), 1.0, 6.0, ((0, 64), (1, 2))),
        "out_weight": centred(arg_keys[3], (D, D), D ** -0.5, 0.125, ((0, 2),)),
        "grad_out": noise_with(arg_keys[4], (SEQ, D), 1.0, 16.0, ((0, 64), (1, 2)), (0, 1, 64, 4.0)),
        "doc_ids": jnp.searchsorted(jnp.cumsum(ragged(arg_keys[5], DOCS, SEQ, SEQ // 2, 0)), jnp.arange(SEQ), side="right").astype(jnp.int32),
    }


def exact_product(form, left, right):
    return jnp.einsum(form, left.astype(jnp.float32), right.astype(jnp.float32), precision=lax.Precision.HIGHEST)

def round_low(array):
    return lax.optimization_barrier(array.astype(jnp.bfloat16)).astype(jnp.float32)

def chain_link(earlier_part, later_part):
    earlier_states, earlier_mark = earlier_part
    later_states, later_mark = later_part
    joined = (later_mark < 0) | (earlier_mark == later_mark)
    merged = later_states + jnp.where(joined, earlier_states, jnp.zeros_like(earlier_states))
    return (merged, jnp.where(later_mark < 0, earlier_mark, later_mark))

def block_terms(query_block, key_block, value_block, grad_block, id_block):
    places = lax.iota(jnp.int32, id_block.shape[0])
    allowed = (places[:, None] >= places[None, :]) & (id_block[:, None] == id_block[None, :])
    attend = exact_product('thd,shd->hts', query_block, key_block)
    attend = round_low(jnp.where(allowed[None], attend, jnp.zeros_like(attend)))
    pulled = exact_product('the,she->hts', grad_block, value_block)
    pulled = round_low(jnp.where(allowed[None], pulled, jnp.zeros_like(pulled)))
    output_part = exact_product('hts,she->the', attend, value_block)
    query_part = exact_product('hts,shd->thd', pulled, key_block)
    key_part = exact_product('hts,thd->shd', pulled, query_block)
    value_part = exact_product('hts,the->she', attend, grad_block)
    return (output_part, query_part, key_part, value_part)

def reference(queries, keys, values, out_weight, grad_out, doc_ids):
    total_rows = queries.shape[0]
    block_rows = min(512, total_rows)
    block_count = total_rows // block_rows
    factor = 1.0 / math.sqrt(HD * total_rows / DOCS)
    grad_heads = exact_product('tj,ej->te', grad_out, out_weight).astype(jnp.bfloat16)

    def split_rows(array):
        return array.reshape(block_count, block_rows, H, HD)
    query_blocks = split_rows(queries)
    key_blocks = split_rows(keys)
    value_blocks = split_rows(values)
    grad_blocks = split_rows(grad_heads)
    id_blocks = doc_ids.reshape(block_count, block_rows)
    empty = (jnp.zeros((H, HD, HD), jnp.float32), jnp.full((), -1, jnp.int32))

    def forward_turn(carried, pieces):
        query_block, key_block, value_block, grad_block, id_block = pieces
        output_part, query_part, key_part, value_part = block_terms(query_block, key_block, value_block, grad_block, id_block)
        state_sum, doc_mark = carried
        joined = (id_block == doc_mark)[:, None, None]
        output_part = output_part + jnp.where(joined, exact_product('thd,hde->the', query_block, state_sum), 0.0)
        query_part = query_part + jnp.where(joined, exact_product('hde,the->thd', state_sum, grad_block), 0.0)
        at_tail = (id_block == id_block[-1]).astype(jnp.float32)[:, None, None]
        element = (exact_product('thd,the->hde', key_block.astype(jnp.float32) * at_tail, value_block), id_block[-1])
        return (chain_link(carried, element), (output_part, query_part, key_part, value_part))
    final_keys, (outputs, query_grads, key_grads, value_grads) = lax.scan(forward_turn, empty, (query_blocks, key_blocks, value_blocks, grad_blocks, id_blocks))

    def reverse_turn(carried, pieces):
        query_block, key_block, value_block, grad_block, id_block = pieces
        state_sum, doc_mark = carried
        joined = (id_block == doc_mark)[:, None, None]
        key_part = jnp.where(joined, exact_product('hde,she->shd', state_sum, value_block), 0.0)
        value_part = jnp.where(joined, exact_product('shd,hde->she', key_block, state_sum), 0.0)
        at_head = (id_block == id_block[0]).astype(jnp.float32)[:, None, None]
        element = (exact_product('thd,the->hde', query_block.astype(jnp.float32) * at_head, grad_block), id_block[0])
        return (chain_link(carried, element), (key_part, value_part))
    final_queries, (key_late, value_late) = lax.scan(reverse_turn, empty, (query_blocks, key_blocks, value_blocks, grad_blocks, id_blocks), reverse=True)
    attn_out = (outputs * factor).astype(jnp.bfloat16).reshape(total_rows, H, HD)
    grad_queries = (query_grads * factor).astype(jnp.bfloat16).reshape(total_rows, H * HD)
    grad_keys = ((key_grads + key_late) * factor).astype(jnp.bfloat16).reshape(total_rows, H * HD)
    grad_values = ((value_grads + value_late) * factor).astype(jnp.bfloat16).reshape(total_rows, H * HD)
    grad_weight = exact_product('tj,the->jhe', grad_out, attn_out) / math.sqrt(total_rows)
    return (grad_queries, grad_keys, grad_values, grad_weight)
```

```python
import math

import jax
import jax.numpy as jnp
from jax import lax
from jax.experimental import pallas as pl
from jax.experimental.pallas import tpu as pltpu
from jax.sharding import PartitionSpec as P

HD = 128
DOCS = 4
SIDE = 4
PLANE = SIDE * SIDE
ROWS = 256
HEADS = 8
WIDTH = HEADS * HD
MODEL = 2 * WIDTH
PIECE = 64
BLOCK = 32
MESH = pl.DeviceIdType.MESH
COLOURS = (((0, 384), 0, 1, 2), ((384, 768), 1, 2, 0), ((768, 1024), 2, 0, 1))
F32 = jnp.float32
BF16 = jnp.bfloat16


def dot(a, b, dims=((1,), (0,))):
    return lax.dot_general(a, b, (dims, ((), ())), preferred_element_type=F32)


NT = ((1,), (1,))
TN = ((0,), (0,))


def kernel(
    factor, weight_factor,
    ids_ref, q_hbm, k_hbm, v_hbm, w_hbm, g_hbm,
    dq_hbm, dk_hbm, dv_hbm, gw_hbm,
    q_v, k_v, v_v, w_v, g_v, gh_v, gt_v,
    idc_v, allow_v, att_v, pul_v, o_v, dq_v, dk_v, dv_v, gw_v,
    ks_v, kr_v, kt_v, kz_v, kp_v, kb_v, s_v,
    qs_v, qr_v, qt_v, qz_v, qp_v, qb_v, t_v,
    gb_v, ab_v, s2_v, r2_v, s3_v, r3_v,
    loc, gx_s, gx_r,
    k1s, k1r, k2s, k2r, k3s, k3r,
    q1s, q1r, q2s, q2r, q3s, q3r,
    gs, gr, fs, fr, as_, ar, b2s, b2r, b3s, b3r,
):
    ctx = lax.axis_index("ctx")
    half = lax.axis_index("head")
    z = ctx // PLANE
    x = (ctx // SIDE) % SIDE
    y = ctx % SIDE
    me = ctx % PLANE
    pos = (z, x, y)

    def plane_peer(k):
        return ((z * PLANE + (me + k) % PLANE), half)

    def axis_peer(axis, d):
        p = [z, x, y]
        p[axis] = (p[axis] + d) % SIDE
        return (p[0] * PLANE + p[1] * SIDE + p[2], half)

    partner = (ctx, 1 - half)

    def remote(src, dst, ssem, rsem, peer):
        return pltpu.make_async_remote_copy(
            src_ref=src, dst_ref=dst, send_sem=ssem, recv_sem=rsem,
            device_id=peer, device_id_type=MESH,
        )

    load_k = pltpu.make_async_copy(k_hbm, k_v, loc.at[0])
    load_v = pltpu.make_async_copy(v_hbm, v_v, loc.at[1])
    load_g = pltpu.make_async_copy(g_hbm, g_v.at[half], loc.at[2])
    load_q = pltpu.make_async_copy(q_hbm, q_v, loc.at[3])
    load_w = pltpu.make_async_copy(w_hbm, w_v, loc.at[4])
    for load in (load_k, load_v, load_g, load_q, load_w):
        load.start()

    barrier = pltpu.get_barrier_semaphore()

    def greet(k, carry):
        pl.semaphore_signal(barrier, inc=1, device_id=plane_peer(k), device_id_type=MESH)
        return carry

    lax.fori_loop(1, PLANE, greet, 0)
    for d in (1, 2, 3):
        pl.semaphore_signal(barrier, inc=1, device_id=axis_peer(0, d), device_id_type=MESH)
    pl.semaphore_signal(barrier, inc=1, device_id=partner, device_id_type=MESH)

    id_row = ids_ref[...].astype(F32)
    id_col = jnp.transpose(jnp.broadcast_to(id_row, (HD, ROWS)))
    idc_v[...] = id_col
    first = id_col[0:1, :]
    last = id_col[ROWS - 1:ROWS, :]
    below = lax.broadcasted_iota(jnp.int32, (ROWS, ROWS), 0) >= lax.broadcasted_iota(
        jnp.int32, (ROWS, ROWS), 1
    )
    same = jnp.concatenate([id_col, id_col], axis=1) == id_row
    allow_v[...] = jnp.where(below & same, 1.0, 0.0).astype(F32)
    marks = jnp.concatenate(
        [jnp.broadcast_to(first, (8, HD)), jnp.broadcast_to(last, (8, HD))], axis=0
    ).astype(BF16)

    def cols(h):
        return pl.ds(pl.multiple_of(h * HD, HD), HD)

    def summarise(a_v, b_v, out_v, edge):
        mask = jnp.where(idc_v[...] == edge, 1.0, 0.0).astype(BF16)

        def one(h, carry):
            state = dot(a_v[:, cols(h)] * mask, b_v[:, cols(h)], TN).astype(BF16)
            out_v[2 * h, 0:PIECE, :] = state[0:PIECE]
            out_v[2 * h + 1, 0:PIECE, :] = state[PIECE:]
            out_v[2 * h, PIECE:, :] = marks
            out_v[2 * h + 1, PIECE:, :] = marks
            return carry

        lax.fori_loop(0, HEADS, one, 0)

    def plane_copies(src, dst, ssem, rsem):
        def make(k):
            return remote(
                src.at[(me + k) % PLANE], dst.at[me], ssem.at[k], rsem.at[k], plane_peer(k)
            )
        return make

    def start_all(make, count):
        def one(k, carry):
            make(k).start()
            return carry
        lax.fori_loop(1, count, one, 0)

    def recv_all(make, count):
        def one(k, carry):
            make(k).wait_recv()
            return carry
        lax.fori_loop(1, count, one, 0)

    def sent_all(make, count):
        def one(k, carry):
            make(k).wait_send()
            return carry
        lax.fori_loop(1, count, one, 0)

    def z_copies(src, dst, ssem, rsem):
        def make(d):
            return remote(src, dst.at[d], ssem.at[d], rsem.at[d], axis_peer(0, d))
        return make

    def scan_plane(recv, part, total, backward):
        order = range(PLANE - 1, -1, -1) if backward else range(PLANE)
        acc = jnp.zeros((PIECE, HD), F32)
        mark = None
        for m in order:
            ids = recv[m, PIECE:, :].astype(F32)
            first_m, last_m = ids[0:1], ids[8:9]
            near, far = (last_m, first_m) if backward else (first_m, last_m)
            item = recv[m, 0:PIECE, :].astype(F32)
            if mark is None:
                part[m] = jnp.zeros((PIECE, HD), F32)
                acc = item
            else:
                part[m] = acc * jnp.where(mark == near, 1.0, 0.0)
                acc = item + acc * jnp.where(mark == far, 1.0, 0.0)
            mark = far
        total[0:PIECE, :] = acc.astype(BF16)
        total[PIECE:, :] = jnp.broadcast_to(mark, (16, HD)).astype(BF16)

    def finish_prefix(recv, part, zrecv, back, backward):
        terms = []
        for d in (1, 2, 3):
            valid = (d > z) if backward else (d <= z)
            keep = jnp.where(valid, 1.0, 0.0)
            terms.append((zrecv[d, 0:PIECE, :].astype(F32) * keep, zrecv[d, PIECE:, :].astype(F32)[0:1]))

        def one(m, carry):
            ids = recv[m, PIECE:, :].astype(F32)
            near = ids[8:9] if backward else ids[0:1]
            value = part[m]
            for term, mark in terms:
                value = value + term * jnp.where(mark == near, 1.0, 0.0)
            back[m] = value.astype(BF16)
            return carry

        lax.fori_loop(0, PLANE, one, 0)

    load_k.wait()
    load_v.wait()
    summarise(k_v, v_v, ks_v, last)
    kr_v[me] = ks_v[me]
    load_g.wait()

    def flip(hf):
        def one(j, carry):
            zz = 2 * hf + j // SIDE
            xx = j % SIDE
            block = jnp.transpose(g_v[hf, :, cols(j)])
            gt_v[zz, xx] = block.reshape(SIDE, BLOCK, ROWS)
            return carry
        lax.fori_loop(0, HEADS, one, 0)

    flip(half)
    pl.semaphore_wait(barrier, PLANE - 1 + 3 + 1)

    give_g = remote(g_v.at[half], g_v.at[half], gx_s, gx_r, partner)
    give_g.start()
    k1 = plane_copies(ks_v, kr_v, k1s, k1r)
    start_all(k1, PLANE)

    def slice_of(colour, q):
        axis = COLOURS[colour][1]
        if axis == 0:
            return gt_v.at[q, pl.ds(2 * half, 2)]
        if axis == 1:
            return gt_v.at[pl.ds(2 * half, 2), q]
        return gt_v.at[pl.ds(2 * half, 2), :, q]

    def g_copy(colour, d):
        axis = COLOURS[colour][1]
        return remote(
            slice_of(colour, (pos[axis] + d) % SIDE),
            gb_v.at[colour, d, pl.ds(2 * half, 2)],
            gs.at[colour, d], gr.at[colour, d], axis_peer(axis, d),
        )

    def g_pass(colour, d):
        part = gb_v.at[colour, d, pl.ds(2 * half, 2)]
        return remote(part, part, fs.at[colour, d], fr.at[colour, d], partner)

    for colour in (1, 2):
        for d in (1, 3, 2):
            g_copy(colour, d).start()

    load_q.wait()

    def attend_head(h, carry):
        a = dot(q_v[:, cols(h)], k_v[:, cols(h)], NT) * allow_v[...]
        a = a.astype(BF16)
        att_v[h] = a
        o_v[:, cols(h)] = dot(a, v_v[:, cols(h)])
        return carry

    lax.fori_loop(0, HEADS, attend_head, 0)

    give_g.wait_recv()
    load_w.wait()

    def grad_chunk(c, carry):
        rows = pl.ds(pl.multiple_of(c * 256, 256), 256)
        value = dot(g_v[0], w_v[rows, 0:WIDTH], NT) + dot(g_v[1], w_v[rows, WIDTH:], NT)
        gh_v[:, rows] = value.astype(BF16)
        return carry

    lax.fori_loop(0, WIDTH // 256, grad_chunk, 0)
    summarise(q_v, gh_v, qs_v, first)
    qr_v[me] = qs_v[me]

    recv_all(k1, PLANE)
    scan_plane(kr_v, kp_v, kt_v, False)
    k2 = z_copies(kt_v, kz_v, k2s, k2r)
    start_all(k2, SIDE)
    q1 = plane_copies(qs_v, qr_v, q1s, q1r)
    start_all(q1, PLANE)

    flip(1 - half)
    for d in (1, 3, 2):
        g_copy(0, d).start()
    for colour in range(3):
        axis = COLOURS[colour][1]
        q = pos[axis]
        if axis == 0:
            gb_v[colour, 0] = gt_v[q]
        elif axis == 1:
            gb_v[colour, 0] = gt_v[:, q]
        else:
            gb_v[colour, 0] = gt_v[:, :, q]

    recv_all(k2, SIDE)
    finish_prefix(kr_v, kp_v, kz_v, kb_v, False)
    k3 = plane_copies(kb_v, s_v, k3s, k3r)
    start_all(k3, PLANE)
    s_v[me] = kb_v[me]

    def pulled_head(h, carry):
        p = dot(gh_v[:, cols(h)], v_v[:, cols(h)], NT) * allow_v[...]
        p = p.astype(BF16)
        dq_v[:, cols(h)] = dot(p, k_v[:, cols(h)])
        dk_v[:, cols(h)] = dot(p, q_v[:, cols(h)], TN)
        dv_v[:, cols(h)] = dot(att_v[h], gh_v[:, cols(h)], TN)
        return carry

    lax.fori_loop(0, HEADS, pulled_head, 0)

    recv_all(q1, PLANE)
    scan_plane(qr_v, qp_v, qt_v, True)
    q2 = z_copies(qt_v, qz_v, q2s, q2r)
    start_all(q2, SIDE)

    recv_all(k3, PLANE)

    def out_head(h, carry):
        keep = jnp.where(idc_v[...] == idc_v[0:1, :], factor, 0.0)
        state = s_v[pl.ds(2 * h, 2)].reshape(HD, HD)
        o = o_v[:, cols(h)] * factor + dot(q_v[:, cols(h)], state) * keep
        ab_v[0, :, cols(h)] = o.astype(BF16)
        return carry

    def a_copy(colour, d):
        (lo, hi), axis = COLOURS[colour][:2]
        return remote(
            ab_v.at[0, :, lo:hi], ab_v.at[d, :, lo:hi],
            as_.at[colour, d], ar.at[colour, d], axis_peer(axis, d),
        )

    for colour in range(3):
        lo, hi = COLOURS[colour][0]
        lax.fori_loop(lo // HD, hi // HD, out_head, 0)
        for d in (1, 3, 2):
            a_copy(colour, d).start()

    recv_all(q2, SIDE)
    finish_prefix(qr_v, qp_v, qz_v, qb_v, True)
    q3 = plane_copies(qb_v, t_v, q3s, q3r)
    start_all(q3, PLANE)
    t_v[me] = qb_v[me]

    for colour in (1, 2, 0):
        for d in (1, 3, 2):
            g_copy(colour, d).wait_recv()
            g_pass(colour, d).start()

    def dq_head(h, carry):
        keep = jnp.where(idc_v[...] == idc_v[0:1, :], factor, 0.0)
        state = s_v[pl.ds(2 * h, 2)].reshape(HD, HD)
        dq = dq_v[:, cols(h)] * factor + dot(gh_v[:, cols(h)], state, NT) * keep
        q_v[:, cols(h)] = dq.astype(BF16)
        return carry

    lax.fori_loop(0, HEADS, dq_head, 0)
    put_q = pltpu.make_async_copy(q_v, dq_hbm, loc.at[5])
    put_q.start()

    def s2_copy(colour, d):
        (lo, hi), _, axis, _ = COLOURS[colour]
        return remote(
            s2_v.at[(pos[axis] + d) % SIDE, :, lo:hi], r2_v.at[d, :, lo:hi],
            b2s.at[colour, d], b2r.at[colour, d], axis_peer(axis, d),
        )

    def s3_copy(colour, d):
        (lo, hi), _, _, axis = COLOURS[colour]
        return remote(
            s3_v.at[(pos[axis] + d) % SIDE, :, lo:hi], r3_v.at[d, :, lo:hi],
            b3s.at[colour, d], b3r.at[colour, d], axis_peer(axis, d),
        )

    for colour in range(3):
        (lo, hi), _, axis, _ = COLOURS[colour]
        for d in (1, 3, 2):
            g_pass(colour, d).wait_recv()
        for d in (1, 3, 2):
            a_copy(colour, d).wait_recv()

        def product(o, carry):
            value = dot(gb_v[colour, 0, o].reshape(128, ROWS), ab_v[0, :, lo:hi])
            for d in (1, 2, 3):
                value = value + dot(gb_v[colour, d, o].reshape(128, ROWS), ab_v[d, :, lo:hi])
            value = value.astype(BF16)
            if axis == 2:
                for i in range(SIDE):
                    s2_v[i, pl.ds(pl.multiple_of(o * BLOCK, BLOCK), BLOCK), lo:hi] = value[
                        i * BLOCK:(i + 1) * BLOCK
                    ]
            else:
                s2_v[o, :, lo:hi] = value
            return carry

        lax.fori_loop(0, SIDE, product, 0)
        for d in (1, 3, 2):
            s2_copy(colour, d).start()

    recv_all(q3, PLANE)

    def kv_head(h, carry):
        keep = jnp.where(idc_v[...] == idc_v[ROWS - 1:ROWS, :], factor, 0.0)
        state = t_v[pl.ds(2 * h, 2)].reshape(HD, HD)
        vh = v_v[:, cols(h)]
        kh = k_v[:, cols(h)]
        dk = dk_v[:, cols(h)] * factor + dot(vh, state, NT) * keep
        dv = dv_v[:, cols(h)] * factor + dot(kh, state) * keep
        k_v[:, cols(h)] = dk.astype(BF16)
        v_v[:, cols(h)] = dv.astype(BF16)
        return carry

    lax.fori_loop(0, HEADS, kv_head, 0)
    put_k = pltpu.make_async_copy(k_v, dk_hbm, loc.at[6])
    put_v = pltpu.make_async_copy(v_v, dv_hbm, loc.at[7])
    put_k.start()
    put_v.start()

    for colour in range(3):
        (lo, hi), _, axis, _ = COLOURS[colour]
        for d in (1, 3, 2):
            s2_copy(colour, d).wait_recv()
        for i in range(SIDE):
            rows = slice(i * BLOCK, (i + 1) * BLOCK)
            value = s2_v[pos[axis], rows, lo:hi].astype(F32)
            for d in (1, 2, 3):
                value = value + r2_v[d, rows, lo:hi].astype(F32)
            s3_v[i, :, lo:hi] = value.astype(BF16)
        for d in (1, 3, 2):
            s3_copy(colour, d).start()

    for colour in range(3):
        (lo, hi), _, _, axis = COLOURS[colour]
        for d in (1, 3, 2):
            s3_copy(colour, d).wait_recv()
        value = s3_v[pos[axis], :, lo:hi].astype(F32)
        for d in (1, 2, 3):
            value = value + r3_v[d, :, lo:hi].astype(F32)
        value = value * weight_factor
        for h in range(lo // HD, hi // HD):
            gw_v[:, h, :] = value[:, h * HD - lo:(h + 1) * HD - lo]
    put_w = pltpu.make_async_copy(gw_v, gw_hbm, loc.at[8])
    put_w.start()

    give_g.wait_send()
    for make in (k1, q1, k3, q3):
        sent_all(make, PLANE)
    for make in (k2, q2):
        sent_all(make, SIDE)
    for colour in range(3):
        for d in (1, 2, 3):
            g_copy(colour, d).wait_send()
            g_pass(colour, d).wait_send()
            a_copy(colour, d).wait_send()
            s2_copy(colour, d).wait_send()
            s3_copy(colour, d).wait_send()
    for put in (put_q, put_k, put_v, put_w):
        put.wait()


def local(queries, keys, values, out_weight, grad_out, doc_ids):
    total_rows = ROWS * lax.axis_size("ctx")
    factor = 1.0 / math.sqrt(HD * total_rows / DOCS)
    weight_factor = 1.0 / math.sqrt(total_rows)
    dma = pltpu.SemaphoreType.DMA

    def vm(*shape, dtype=BF16):
        return pltpu.VMEM(shape, dtype)

    prefix = [
        vm(PLANE, PIECE + 16, HD), vm(PLANE, PIECE + 16, HD), vm(PIECE + 16, HD),
        vm(SIDE, PIECE + 16, HD), vm(PLANE, PIECE, HD, dtype=F32), vm(PLANE, PIECE, HD),
        vm(PLANE, PIECE, HD),
    ]
    prefix_sems = [dma((PLANE,)), dma((PLANE,)), dma((SIDE,)), dma((SIDE,)), dma((PLANE,)), dma((PLANE,))]
    flat = (ROWS, WIDTH)
    scratch = [
        vm(*flat), vm(*flat), vm(*flat), vm(WIDTH, MODEL), vm(2, *flat), vm(*flat),
        vm(SIDE, SIDE, SIDE, BLOCK, ROWS),
        vm(ROWS, HD, dtype=F32), vm(ROWS, ROWS, dtype=F32), vm(HEADS, ROWS, ROWS),
        vm(8, 128), vm(*flat, dtype=F32), vm(*flat, dtype=F32), vm(*flat, dtype=F32),
        vm(*flat, dtype=F32), vm(BLOCK, HEADS, HD, dtype=F32),
        *prefix, *prefix,
        vm(3, SIDE, SIDE, SIDE, BLOCK, ROWS), vm(SIDE, *flat),
        vm(SIDE, 128, WIDTH), vm(SIDE, 128, WIDTH), vm(SIDE, BLOCK, WIDTH), vm(SIDE, BLOCK, WIDTH),
        dma((9,)), dma(()), dma(()),
        *prefix_sems, *prefix_sems,
        *[dma((3, SIDE)) for _ in range(10)],
    ]
    any_space = pl.BlockSpec(memory_space=pl.ANY)
    shape = jax.ShapeDtypeStruct
    return pl.pallas_call(
        lambda *refs: kernel(factor, weight_factor, *refs),
        out_shape=(
            shape(flat, BF16), shape(flat, BF16), shape(flat, BF16),
            shape((BLOCK, HEADS, HD), F32),
        ),
        in_specs=[pl.BlockSpec(memory_space=pltpu.VMEM)] + [any_space] * 5,
        out_specs=(any_space,) * 4,
        scratch_shapes=scratch,
        compiler_params=pltpu.CompilerParams(collective_id=0, has_side_effects=True),
        name="linear_attention_backward",
    )(doc_ids.reshape(1, ROWS), queries, keys, values, out_weight, grad_out)


def solution(mesh):
    return jax.shard_map(
        local,
        mesh=mesh,
        in_specs=(
            P("ctx", "head"),
            P("ctx", "head"),
            P("ctx", "head"),
            P("head", None),
            P("ctx", "head"),
            P("ctx"),
        ),
        out_specs=(P("ctx", "head"), P("ctx", "head"), P("ctx", "head"), P("ctx", "head", None)),
        check_vma=False,
    )
```

```python
import math

import jax
import jax.numpy as jnp
from jax import lax
from jax.experimental import pallas as pl
from jax.experimental.pallas import tpu as pltpu
from jax.sharding import PartitionSpec as P

HD = 128
DOCS = 4
SIDE = 4
PLANE = SIDE * SIDE
ROWS = 256
HEADS = 8
WIDTH = HEADS * HD
MODEL = 2 * WIDTH
PIECE = 64
BLOCK = 32
MESH = pl.DeviceIdType.MESH
COLOURS = (((0, 384), 0, 1, 2), ((384, 768), 1, 2, 0), ((768, 1024), 2, 0, 1))
F32 = jnp.float32
BF16 = jnp.bfloat16


def dot(a, b, dims=((1,), (0,))):
    return lax.dot_general(a, b, (dims, ((), ())), preferred_element_type=F32)


NT = ((1,), (1,))
TN = ((0,), (0,))


def kernel(
    factor, weight_factor,
    ids_ref, q_hbm, k_hbm, v_hbm, w_hbm, g_hbm,
    dq_hbm, dk_hbm, dv_hbm, gw_hbm,
    q_v, k_v, v_v, w_v, g_v, gh_v, gt_v,
    idc_v, allow_v, att_v, o_v, dq_v, dk_v, dv_v, gw_v,
    ks_v, kr_v, kt_v, kz_v, kp_v, kb_v, s_v,
    qs_v, qr_v, qt_v, qz_v, qp_v, qb_v, t_v,
    gb_v, ab_v, s2_v, r2_v, s3_v, r3_v,
    loc, gx_s, gx_r,
    k1s, k1r, k2s, k2r, k3s, k3r,
    q1s, q1r, q2s, q2r, q3s, q3r,
    gs, gr, fs, fr, as_, ar, b2s, b2r, b3s, b3r,
):
    ctx = lax.axis_index("ctx")
    half = lax.axis_index("head")
    z = ctx // PLANE
    x = (ctx // SIDE) % SIDE
    y = ctx % SIDE
    me = ctx % PLANE
    pos = (z, x, y)

    def plane_peer(k):
        return ((z * PLANE + (me + k) % PLANE), half)

    def axis_peer(axis, d):
        p = [z, x, y]
        p[axis] = (p[axis] + d) % SIDE
        return (p[0] * PLANE + p[1] * SIDE + p[2], half)

    partner = (ctx, 1 - half)

    def remote(src, dst, ssem, rsem, peer):
        return pltpu.make_async_remote_copy(
            src_ref=src, dst_ref=dst, send_sem=ssem, recv_sem=rsem,
            device_id=peer, device_id_type=MESH,
        )

    load_k = pltpu.make_async_copy(k_hbm, k_v, loc.at[0])
    load_v = pltpu.make_async_copy(v_hbm, v_v, loc.at[1])
    load_g = pltpu.make_async_copy(g_hbm, g_v.at[half], loc.at[2])
    load_q = pltpu.make_async_copy(q_hbm, q_v, loc.at[3])
    load_w = pltpu.make_async_copy(w_hbm, w_v, loc.at[4])
    for load in (load_k, load_v, load_g, load_q, load_w):
        load.start()

    barrier = pltpu.get_barrier_semaphore()

    def greet(k, carry):
        pl.semaphore_signal(barrier, inc=1, device_id=plane_peer(k), device_id_type=MESH)
        return carry

    lax.fori_loop(1, PLANE, greet, 0)
    for d in (1, 2, 3):
        pl.semaphore_signal(barrier, inc=1, device_id=axis_peer(0, d), device_id_type=MESH)
    pl.semaphore_signal(barrier, inc=1, device_id=partner, device_id_type=MESH)

    id_row = ids_ref[...].astype(F32)
    id_col = jnp.transpose(jnp.broadcast_to(id_row, (HD, ROWS)))
    idc_v[...] = id_col
    first = id_col[0:1, :]
    last = id_col[ROWS - 1:ROWS, :]
    below = lax.broadcasted_iota(jnp.int32, (ROWS, ROWS), 0) >= lax.broadcasted_iota(
        jnp.int32, (ROWS, ROWS), 1
    )
    same = jnp.concatenate([id_col, id_col], axis=1) == id_row
    allow_v[...] = jnp.where(below & same, 1.0, 0.0).astype(F32)
    marks = jnp.concatenate(
        [jnp.broadcast_to(first, (8, HD)), jnp.broadcast_to(last, (8, HD))], axis=0
    ).astype(BF16)

    def cols(h):
        return pl.ds(pl.multiple_of(h * HD, HD), HD)

    def summarise(a_v, b_v, out_v, edge):
        mask = jnp.where(idc_v[...] == edge, 1.0, 0.0).astype(BF16)

        def one(h, carry):
            state = dot(a_v[:, cols(h)] * mask, b_v[:, cols(h)], TN).astype(BF16)
            out_v[2 * h, 0:PIECE, :] = state[0:PIECE]
            out_v[2 * h + 1, 0:PIECE, :] = state[PIECE:]
            out_v[2 * h, PIECE:, :] = marks
            out_v[2 * h + 1, PIECE:, :] = marks
            return carry

        lax.fori_loop(0, HEADS, one, 0, unroll=True)

    def plane_copies(src, dst, ssem, rsem):
        def make(k):
            return remote(
                src.at[(me + k) % PLANE], dst.at[me], ssem.at[k], rsem.at[k], plane_peer(k)
            )
        return make

    def start_all(make, count):
        def one(k, carry):
            make(k).start()
            return carry
        lax.fori_loop(1, count, one, 0)

    def recv_all(make, count):
        def one(k, carry):
            make(k).wait_recv()
            return carry
        lax.fori_loop(1, count, one, 0)

    def sent_all(make, count):
        def one(k, carry):
            make(k).wait_send()
            return carry
        lax.fori_loop(1, count, one, 0)

    def z_copies(src, dst, ssem, rsem):
        def make(d):
            return remote(src, dst.at[d], ssem.at[d], rsem.at[d], axis_peer(0, d))
        return make

    def scan_plane(recv, part, total, backward):
        order = range(PLANE - 1, -1, -1) if backward else range(PLANE)
        acc = jnp.zeros((PIECE, HD), F32)
        mark = None
        for m in order:
            ids = recv[m, PIECE:, :].astype(F32)
            first_m, last_m = ids[0:1], ids[8:9]
            near, far = (last_m, first_m) if backward else (first_m, last_m)
            item = recv[m, 0:PIECE, :].astype(F32)
            if mark is None:
                part[m] = jnp.zeros((PIECE, HD), F32)
                acc = item
            else:
                part[m] = acc * jnp.where(mark == near, 1.0, 0.0)
                acc = item + acc * jnp.where(mark == far, 1.0, 0.0)
            mark = far
        total[0:PIECE, :] = acc.astype(BF16)
        total[PIECE:, :] = jnp.broadcast_to(mark, (16, HD)).astype(BF16)

    def finish_prefix(recv, part, zrecv, back, backward):
        terms = []
        for d in (1, 2, 3):
            valid = (d > z) if backward else (d <= z)
            keep = jnp.where(valid, 1.0, 0.0)
            terms.append((zrecv[d, 0:PIECE, :].astype(F32) * keep, zrecv[d, PIECE:, :].astype(F32)[0:1]))

        def one(m, carry):
            ids = recv[m, PIECE:, :].astype(F32)
            near = ids[8:9] if backward else ids[0:1]
            value = part[m]
            for term, mark in terms:
                value = value + term * jnp.where(mark == near, 1.0, 0.0)
            back[m] = value.astype(BF16)
            return carry

        lax.fori_loop(0, PLANE, one, 0, unroll=True)

    def flip(hf):
        def one(j, carry):
            zz = 2 * hf + j // SIDE
            xx = j % SIDE
            block = jnp.transpose(g_v[hf, :, cols(j)])
            gt_v[zz, xx] = block.reshape(SIDE, BLOCK, ROWS)
            return carry
        lax.fori_loop(0, HEADS, one, 0, unroll=True)

    def attend_head(h, carry):
        a = dot(q_v[:, cols(h)], k_v[:, cols(h)], NT) * allow_v[...]
        a = a.astype(BF16)
        att_v[h] = a
        o_v[:, cols(h)] = dot(a, v_v[:, cols(h)])
        return carry

    def grad_chunk(c, carry):
        rows = pl.ds(pl.multiple_of(c * 256, 256), 256)
        value = dot(g_v[0], w_v[rows, 0:WIDTH], NT) + dot(g_v[1], w_v[rows, WIDTH:], NT)
        gh_v[:, rows] = value.astype(BF16)
        return carry

    def pulled_head(h, carry):
        p = dot(gh_v[:, cols(h)], v_v[:, cols(h)], NT) * allow_v[...]
        p = p.astype(BF16)
        dq_v[:, cols(h)] = dot(p, k_v[:, cols(h)])
        dk_v[:, cols(h)] = dot(p, q_v[:, cols(h)], TN)
        dv_v[:, cols(h)] = dot(att_v[h], gh_v[:, cols(h)], TN)
        return carry

    def out_head(h, carry):
        keep = jnp.where(idc_v[...] == idc_v[0:1, :], factor, 0.0)
        state = s_v[pl.ds(2 * h, 2)].reshape(HD, HD)
        o = o_v[:, cols(h)] * factor + dot(q_v[:, cols(h)], state) * keep
        ab_v[0, :, cols(h)] = o.astype(BF16)
        return carry

    def dq_head(h, carry):
        keep = jnp.where(idc_v[...] == idc_v[0:1, :], factor, 0.0)
        state = s_v[pl.ds(2 * h, 2)].reshape(HD, HD)
        dq = dq_v[:, cols(h)] * factor + dot(gh_v[:, cols(h)], state, NT) * keep
        q_v[:, cols(h)] = dq.astype(BF16)
        return carry

    def kv_head(h, carry):
        keep = jnp.where(idc_v[...] == idc_v[ROWS - 1:ROWS, :], factor, 0.0)
        state = t_v[pl.ds(2 * h, 2)].reshape(HD, HD)
        vh = v_v[:, cols(h)]
        kh = k_v[:, cols(h)]
        dk = dk_v[:, cols(h)] * factor + dot(vh, state, NT) * keep
        dv = dv_v[:, cols(h)] * factor + dot(kh, state) * keep
        k_v[:, cols(h)] = dk.astype(BF16)
        v_v[:, cols(h)] = dv.astype(BF16)
        return carry

    give_g = remote(g_v.at[half], g_v.at[half], gx_s, gx_r, partner)
    k1 = plane_copies(ks_v, kr_v, k1s, k1r)
    k2 = z_copies(kt_v, kz_v, k2s, k2r)
    k3 = plane_copies(kb_v, s_v, k3s, k3r)
    q1 = plane_copies(qs_v, qr_v, q1s, q1r)
    q2 = z_copies(qt_v, qz_v, q2s, q2r)
    q3 = plane_copies(qb_v, t_v, q3s, q3r)

    def slice_of(colour, q):
        axis = COLOURS[colour][1]
        if axis == 0:
            return gt_v.at[q, pl.ds(2 * half, 2)]
        if axis == 1:
            return gt_v.at[pl.ds(2 * half, 2), q]
        return gt_v.at[pl.ds(2 * half, 2), :, q]

    def g_copy(colour, d):
        axis = COLOURS[colour][1]
        return remote(
            slice_of(colour, (pos[axis] + d) % SIDE),
            gb_v.at[colour, d, pl.ds(2 * half, 2)],
            gs.at[colour, d], gr.at[colour, d], axis_peer(axis, d),
        )

    def g_pass(colour, d):
        part = gb_v.at[colour, d, pl.ds(2 * half, 2)]
        return remote(part, part, fs.at[colour, d], fr.at[colour, d], partner)

    def a_copy(colour, d):
        (lo, hi), axis = COLOURS[colour][:2]
        return remote(
            ab_v.at[0, :, lo:hi], ab_v.at[d, :, lo:hi],
            as_.at[colour, d], ar.at[colour, d], axis_peer(axis, d),
        )

    def s2_copy(colour, d):
        (lo, hi), _, axis, _ = COLOURS[colour]
        return remote(
            s2_v.at[(pos[axis] + d) % SIDE, :, lo:hi], r2_v.at[d, :, lo:hi],
            b2s.at[colour, d], b2r.at[colour, d], axis_peer(axis, d),
        )

    def s3_copy(colour, d):
        (lo, hi), _, _, axis = COLOURS[colour]
        return remote(
            s3_v.at[(pos[axis] + d) % SIDE, :, lo:hi], r3_v.at[d, :, lo:hi],
            b3s.at[colour, d], b3r.at[colour, d], axis_peer(axis, d),
        )

    def product(colour):
        (lo, hi), _, axis, _ = COLOURS[colour]
        for d in (1, 3, 2):
            g_pass(colour, d).wait_recv()
        for d in (1, 3, 2):
            a_copy(colour, d).wait_recv()
        for o in range(SIDE):
            value = dot(gb_v[colour, 0, o].reshape(128, ROWS), ab_v[0, :, lo:hi])
            for d in (1, 2, 3):
                value = value + dot(gb_v[colour, d, o].reshape(128, ROWS), ab_v[d, :, lo:hi])
            value = value.astype(BF16)
            if axis == 2:
                for i in range(SIDE):
                    s2_v[i, o * BLOCK:(o + 1) * BLOCK, lo:hi] = value[i * BLOCK:(i + 1) * BLOCK]
            else:
                s2_v[o, :, lo:hi] = value
        for d in (1, 3, 2):
            s2_copy(colour, d).start()

    def own_slices():
        gb_v[0, 0] = gt_v[z]
        gb_v[1, 0] = gt_v[:, x]
        gb_v[2, 0] = gt_v[:, :, y]

    def pass_on(colour):
        for d in (1, 3, 2):
            g_copy(colour, d).wait_recv()
            g_pass(colour, d).start()

    def send_g(colour):
        for d in (1, 3, 2):
            g_copy(colour, d).start()

    load_k.wait()
    load_v.wait()
    summarise(k_v, v_v, ks_v, last)
    kr_v[me] = ks_v[me]
    load_q.wait()
    lax.fori_loop(0, HEADS, attend_head, 0, unroll=True)
    load_g.wait()
    flip(half)
    pl.semaphore_wait(barrier, PLANE - 1 + 3 + 1)

    start_all(k1, PLANE)
    give_g.start()
    send_g(1)
    send_g(2)
    give_g.wait_recv()
    load_w.wait()
    lax.fori_loop(0, WIDTH // 256, grad_chunk, 0, unroll=True)
    summarise(q_v, gh_v, qs_v, first)
    qr_v[me] = qs_v[me]
    flip(1 - half)
    recv_all(k1, PLANE)
    scan_plane(kr_v, kp_v, kt_v, False)
    start_all(k2, SIDE)
    send_g(0)
    own_slices()
    recv_all(k2, SIDE)
    finish_prefix(kr_v, kp_v, kz_v, kb_v, False)
    start_all(k3, PLANE)
    s_v[me] = kb_v[me]
    start_all(q1, PLANE)
    lax.fori_loop(0, HEADS, pulled_head, 0, unroll=True)

    recv_all(k3, PLANE)
    for colour in range(3):
        lo, hi = COLOURS[colour][0]
        lax.fori_loop(lo // HD, hi // HD, out_head, 0, unroll=True)
        for d in (1, 3, 2):
            a_copy(colour, d).start()
    recv_all(q1, PLANE)
    scan_plane(qr_v, qp_v, qt_v, True)
    start_all(q2, SIDE)
    pass_on(1)
    pass_on(2)
    pass_on(0)
    recv_all(q2, SIDE)
    finish_prefix(qr_v, qp_v, qz_v, qb_v, True)
    t_v[me] = qb_v[me]
    lax.fori_loop(0, HEADS, dq_head, 0, unroll=True)
    put_q = pltpu.make_async_copy(q_v, dq_hbm, loc.at[5])
    put_q.start()
    for colour in range(3):
        product(colour)
    start_all(q3, PLANE)
    for colour in range(3):
        (lo, hi), _, axis, _ = COLOURS[colour]
        for d in (1, 3, 2):
            s2_copy(colour, d).wait_recv()
        for i in range(SIDE):
            rows = slice(i * BLOCK, (i + 1) * BLOCK)
            value = s2_v[pos[axis], rows, lo:hi].astype(F32)
            for d in (1, 2, 3):
                value = value + r2_v[d, rows, lo:hi].astype(F32)
            s3_v[i, :, lo:hi] = value.astype(BF16)
        for d in (1, 3, 2):
            s3_copy(colour, d).start()
    recv_all(q3, PLANE)
    lax.fori_loop(0, HEADS, kv_head, 0, unroll=True)
    put_k = pltpu.make_async_copy(k_v, dk_hbm, loc.at[6])
    put_v = pltpu.make_async_copy(v_v, dv_hbm, loc.at[7])
    put_k.start()
    put_v.start()
    for colour in range(3):
        (lo, hi), _, _, axis = COLOURS[colour]
        for d in (1, 3, 2):
            s3_copy(colour, d).wait_recv()
        value = s3_v[pos[axis], :, lo:hi].astype(F32)
        for d in (1, 2, 3):
            value = value + r3_v[d, :, lo:hi].astype(F32)
        value = value * weight_factor
        for h in range(lo // HD, hi // HD):
            gw_v[:, h, :] = value[:, h * HD - lo:(h + 1) * HD - lo]
    put_w = pltpu.make_async_copy(gw_v, gw_hbm, loc.at[8])
    put_w.start()

    give_g.wait_send()
    for make in (k1, q1, k3, q3):
        sent_all(make, PLANE)
    for make in (k2, q2):
        sent_all(make, SIDE)
    for colour in range(3):
        for d in (1, 2, 3):
            g_copy(colour, d).wait_send()
            g_pass(colour, d).wait_send()
            a_copy(colour, d).wait_send()
            s2_copy(colour, d).wait_send()
            s3_copy(colour, d).wait_send()
    for put in (put_q, put_k, put_v, put_w):
        put.wait()


def put_out(a, b, c, e, oa, ob, oc, oe, va, vb, vc, ve, into, out):
    gets = [
        pltpu.make_async_copy(s, v, into.at[i])
        for i, (s, v) in enumerate(((a, va), (b, vb), (c, vc), (e, ve)))
    ]
    puts = [
        pltpu.make_async_copy(v, o, out.at[i])
        for i, (v, o) in enumerate(((va, oa), (vb, ob), (vc, oc), (ve, oe)))
    ]
    for get in gets:
        get.start()
    for get, put in zip(gets, puts):
        get.wait()
        put.start()
    for put in puts:
        put.wait()


def local(queries, keys, values, out_weight, grad_out, doc_ids):
    total_rows = ROWS * lax.axis_size("ctx")
    factor = 1.0 / math.sqrt(HD * total_rows / DOCS)
    weight_factor = 1.0 / math.sqrt(total_rows)
    dma = pltpu.SemaphoreType.DMA

    def vm(*shape, dtype=BF16):
        return pltpu.VMEM(shape, dtype)

    prefix = [
        vm(PLANE, PIECE + 16, HD), vm(PLANE, PIECE + 16, HD), vm(PIECE + 16, HD),
        vm(SIDE, PIECE + 16, HD), vm(PLANE, PIECE, HD, dtype=F32), vm(PLANE, PIECE, HD),
        vm(PLANE, PIECE, HD),
    ]
    prefix_sems = [dma((PLANE,)), dma((PLANE,)), dma((SIDE,)), dma((SIDE,)), dma((PLANE,)), dma((PLANE,))]
    flat = (ROWS, WIDTH)
    scratch = [
        vm(*flat), vm(*flat), vm(*flat), vm(WIDTH, MODEL), vm(2, *flat), vm(*flat),
        vm(SIDE, SIDE, SIDE, BLOCK, ROWS),
        vm(ROWS, HD, dtype=F32), vm(ROWS, ROWS, dtype=F32), vm(HEADS, ROWS, ROWS),
        vm(*flat, dtype=F32), vm(*flat, dtype=F32), vm(*flat, dtype=F32),
        vm(*flat, dtype=F32), vm(BLOCK, HEADS, HD, dtype=F32),
        *prefix, *prefix,
        vm(3, SIDE, SIDE, SIDE, BLOCK, ROWS), vm(SIDE, *flat),
        vm(SIDE, 128, WIDTH), vm(SIDE, 128, WIDTH), vm(SIDE, BLOCK, WIDTH), vm(SIDE, BLOCK, WIDTH),
        dma((9,)), dma(()), dma(()),
        *prefix_sems, *prefix_sems,
        *[dma((3, SIDE)) for _ in range(10)],
    ]
    any_space = pl.BlockSpec(memory_space=pl.ANY)
    shape = jax.ShapeDtypeStruct
    outs = (
        shape(flat, BF16), shape(flat, BF16), shape(flat, BF16), shape((BLOCK, HEADS, HD), F32),
    )
    results = pl.pallas_call(
        lambda *refs: kernel(factor, weight_factor, *refs),
        out_shape=outs,
        in_specs=[pl.BlockSpec(memory_space=pltpu.VMEM)] + [any_space] * 5,
        out_specs=(any_space,) * 4,
        scratch_shapes=scratch,
        compiler_params=pltpu.CompilerParams(collective_id=0, has_side_effects=True),
        name="linear_attention_backward",
    )(doc_ids.reshape(1, ROWS), queries, keys, values, out_weight, grad_out)
    return pl.pallas_call(
        put_out,
        out_shape=outs,
        in_specs=[any_space] * 4,
        out_specs=(any_space,) * 4,
        scratch_shapes=[
            vm(*flat), vm(*flat), vm(*flat), vm(BLOCK, HEADS, HD, dtype=F32), dma((4,)), dma((4,)),
        ],
        name="results",
    )(*results)


def solution(mesh):
    return jax.shard_map(
        local,
        mesh=mesh,
        in_specs=(
            P("ctx", "head"),
            P("ctx", "head"),
            P("ctx", "head"),
            P("head", None),
            P("ctx", "head"),
            P("ctx"),
        ),
        out_specs=(P("ctx", "head"), P("ctx", "head"), P("ctx", "head"), P("ctx", "head", None)),
        check_vma=False,
    )
```

```python
import math

import jax
import jax.numpy as jnp
from jax import lax
from jax.experimental import pallas as pl
from jax.experimental.pallas import tpu as pltpu
from jax.sharding import PartitionSpec as P

HD = 128
DOCS = 4
SIDE = 4
PLANE = SIDE * SIDE
ROWS = 256
HEADS = 8
WIDTH = HEADS * HD
MODEL = 2 * WIDTH
PIECE = 64
BLOCK = 32
MESH = pl.DeviceIdType.MESH
COLOURS = (((0, 384), 0, 1, 2), ((384, 768), 1, 2, 0), ((768, 1024), 2, 0, 1))
UNITS = (
    (0, 0, 256), (1, 384, 640), (2, 768, 896), (0, 256, 384), (1, 640, 768), (2, 896, 1024),
)
F32 = jnp.float32
BF16 = jnp.bfloat16


def dot(a, b, dims=((1,), (0,))):
    return lax.dot_general(a, b, (dims, ((), ())), preferred_element_type=F32)


NT = ((1,), (1,))
TN = ((0,), (0,))


def kernel(
    factor, weight_factor,
    ids_ref, q_hbm, k_hbm, v_hbm, w_hbm, g_hbm,
    dq_hbm, dk_hbm, dv_hbm, gw_hbm,
    q_v, k_v, v_v, w_v, g_v, gh_v, gt_v,
    idc_v, allow_v, att_v, o_v, dq_v, dk_v, dv_v, gw_v,
    ks_v, kr_v, kt_v, kz_v, kp_v, kb_v, s_v,
    qs_v, qr_v, qt_v, qz_v, qp_v, qb_v, t_v,
    gb_v, ab_v, s2_v, r2_v, s3_v, r3_v,
    loc, gx_s, gx_r,
    k1s, k1r, k2s, k2r, k3s, k3r,
    q1s, q1r, q2s, q2r, q3s, q3r,
    gs, gr, fs, fr, as_, ar, b2s, b2r, b3s, b3r,
):
    ctx = lax.axis_index("ctx")
    half = lax.axis_index("head")
    z = ctx // PLANE
    x = (ctx // SIDE) % SIDE
    y = ctx % SIDE
    me = ctx % PLANE
    pos = (z, x, y)

    def plane_peer(k):
        return ((z * PLANE + (me + k) % PLANE), half)

    def axis_peer(axis, d):
        p = [z, x, y]
        p[axis] = (p[axis] + d) % SIDE
        return (p[0] * PLANE + p[1] * SIDE + p[2], half)

    partner = (ctx, 1 - half)

    def remote(src, dst, ssem, rsem, peer):
        return pltpu.make_async_remote_copy(
            src_ref=src, dst_ref=dst, send_sem=ssem, recv_sem=rsem,
            device_id=peer, device_id_type=MESH,
        )

    load_k = pltpu.make_async_copy(k_hbm, k_v, loc.at[0])
    load_v = pltpu.make_async_copy(v_hbm, v_v, loc.at[1])
    load_g = pltpu.make_async_copy(g_hbm, g_v.at[half], loc.at[2])
    load_q = pltpu.make_async_copy(q_hbm, q_v, loc.at[3])
    load_w = pltpu.make_async_copy(w_hbm, w_v, loc.at[4])
    for load in (load_k, load_v, load_g, load_q, load_w):
        load.start()

    barrier = pltpu.get_barrier_semaphore()

    def greet(k, carry):
        pl.semaphore_signal(barrier, inc=1, device_id=plane_peer(k), device_id_type=MESH)
        return carry

    lax.fori_loop(1, PLANE, greet, 0)
    for d in (1, 2, 3):
        pl.semaphore_signal(barrier, inc=1, device_id=axis_peer(0, d), device_id_type=MESH)
    pl.semaphore_signal(barrier, inc=1, device_id=partner, device_id_type=MESH)

    id_row = ids_ref[...].astype(F32)
    id_col = jnp.transpose(jnp.broadcast_to(id_row, (HD, ROWS)))
    idc_v[...] = id_col
    first = id_col[0:1, :]
    last = id_col[ROWS - 1:ROWS, :]
    below = lax.broadcasted_iota(jnp.int32, (ROWS, ROWS), 0) >= lax.broadcasted_iota(
        jnp.int32, (ROWS, ROWS), 1
    )
    same = jnp.concatenate([id_col, id_col], axis=1) == id_row
    allow_v[...] = jnp.where(below & same, 1.0, 0.0).astype(F32)
    marks = jnp.concatenate(
        [jnp.broadcast_to(first, (8, HD)), jnp.broadcast_to(last, (8, HD))], axis=0
    ).astype(BF16)

    def cols(h):
        return pl.ds(pl.multiple_of(h * HD, HD), HD)

    def summarise(a_v, b_v, out_v, edge):
        mask = jnp.where(idc_v[...] == edge, 1.0, 0.0).astype(BF16)

        def one(h, carry):
            state = dot(a_v[:, cols(h)] * mask, b_v[:, cols(h)], TN).astype(BF16)
            out_v[2 * h, 0:PIECE, :] = state[0:PIECE]
            out_v[2 * h + 1, 0:PIECE, :] = state[PIECE:]
            out_v[2 * h, PIECE:, :] = marks
            out_v[2 * h + 1, PIECE:, :] = marks
            return carry

        lax.fori_loop(0, HEADS, one, 0, unroll=True)

    def plane_copies(src, dst, ssem, rsem):
        def make(k):
            return remote(
                src.at[(me + k) % PLANE], dst.at[me], ssem.at[k], rsem.at[k], plane_peer(k)
            )
        return make

    def start_all(make, count):
        def one(k, carry):
            make(k).start()
            return carry
        lax.fori_loop(1, count, one, 0)

    def recv_all(make, count):
        def one(k, carry):
            make(k).wait_recv()
            return carry
        lax.fori_loop(1, count, one, 0)

    def sent_all(make, count):
        def one(k, carry):
            make(k).wait_send()
            return carry
        lax.fori_loop(1, count, one, 0)

    def z_copies(src, dst, ssem, rsem):
        def make(d):
            return remote(src, dst.at[d], ssem.at[d], rsem.at[d], axis_peer(0, d))
        return make

    def scan_plane(recv, part, total, backward):
        order = range(PLANE - 1, -1, -1) if backward else range(PLANE)
        acc = jnp.zeros((PIECE, HD), F32)
        mark = None
        for m in order:
            ids = recv[m, PIECE:, :].astype(F32)
            first_m, last_m = ids[0:1], ids[8:9]
            near, far = (last_m, first_m) if backward else (first_m, last_m)
            item = recv[m, 0:PIECE, :].astype(F32)
            if mark is None:
                part[m] = jnp.zeros((PIECE, HD), F32)
                acc = item
            else:
                part[m] = acc * jnp.where(mark == near, 1.0, 0.0)
                acc = item + acc * jnp.where(mark == far, 1.0, 0.0)
            mark = far
        total[0:PIECE, :] = acc.astype(BF16)
        total[PIECE:, :] = jnp.broadcast_to(mark, (16, HD)).astype(BF16)

    def finish_prefix(recv, part, zrecv, back, backward, make=None):
        terms = []
        for d in (1, 2, 3):
            valid = (d > z) if backward else (d <= z)
            keep = jnp.where(valid, 1.0, 0.0)
            terms.append((zrecv[d, 0:PIECE, :].astype(F32) * keep, zrecv[d, PIECE:, :].astype(F32)[0:1]))

        def one(k, carry):
            m = (me + k) % PLANE
            ids = recv[m, PIECE:, :].astype(F32)
            near = ids[8:9] if backward else ids[0:1]
            value = part[m]
            for term, mark in terms:
                value = value + term * jnp.where(mark == near, 1.0, 0.0)
            back[m] = value.astype(BF16)
            return carry

        def both(k, carry):
            one(k, carry)
            if make is not None:
                make(k).start()
            return carry

        lax.fori_loop(1, PLANE, both, 0, unroll=True)
        one(0, 0)

    def flip(hf):
        def one(j, carry):
            zz = 2 * hf + j // SIDE
            xx = j % SIDE
            block = jnp.transpose(g_v[hf, :, cols(j)])
            gt_v[zz, xx] = block.reshape(SIDE, BLOCK, ROWS)
            return carry
        lax.fori_loop(0, HEADS, one, 0, unroll=True)

    def attend_head(h, carry):
        a = dot(q_v[:, cols(h)], k_v[:, cols(h)], NT) * allow_v[...]
        a = a.astype(BF16)
        att_v[h] = a
        o_v[:, cols(h)] = dot(a, v_v[:, cols(h)])
        return carry

    def grad_chunk(c, carry):
        rows = pl.ds(pl.multiple_of(c * 256, 256), 256)
        value = dot(g_v[0], w_v[rows, 0:WIDTH], NT) + dot(g_v[1], w_v[rows, WIDTH:], NT)
        gh_v[:, rows] = value.astype(BF16)
        return carry

    def pulled_head(h, carry):
        p = dot(gh_v[:, cols(h)], v_v[:, cols(h)], NT) * allow_v[...]
        p = p.astype(BF16)
        dq_v[:, cols(h)] = dot(p, k_v[:, cols(h)])
        dk_v[:, cols(h)] = dot(p, q_v[:, cols(h)], TN)
        dv_v[:, cols(h)] = dot(att_v[h], gh_v[:, cols(h)], TN)
        return carry

    def out_head(h, carry):
        keep = jnp.where(idc_v[...] == idc_v[0:1, :], factor, 0.0)
        state = s_v[pl.ds(2 * h, 2)].reshape(HD, HD)
        o = o_v[:, cols(h)] * factor + dot(q_v[:, cols(h)], state) * keep
        ab_v[0, :, cols(h)] = o.astype(BF16)
        return carry

    def dq_head(h, carry):
        keep = jnp.where(idc_v[...] == idc_v[0:1, :], factor, 0.0)
        state = s_v[pl.ds(2 * h, 2)].reshape(HD, HD)
        dq = dq_v[:, cols(h)] * factor + dot(gh_v[:, cols(h)], state, NT) * keep
        q_v[:, cols(h)] = dq.astype(BF16)
        return carry

    def kv_head(h, carry):
        keep = jnp.where(idc_v[...] == idc_v[ROWS - 1:ROWS, :], factor, 0.0)
        state = t_v[pl.ds(2 * h, 2)].reshape(HD, HD)
        vh = v_v[:, cols(h)]
        kh = k_v[:, cols(h)]
        dk = dk_v[:, cols(h)] * factor + dot(vh, state, NT) * keep
        dv = dv_v[:, cols(h)] * factor + dot(kh, state) * keep
        k_v[:, cols(h)] = dk.astype(BF16)
        v_v[:, cols(h)] = dv.astype(BF16)
        return carry

    give_g = remote(g_v.at[half], g_v.at[half], gx_s, gx_r, partner)
    k1 = plane_copies(ks_v, kr_v, k1s, k1r)
    k2 = z_copies(kt_v, kz_v, k2s, k2r)
    k3 = plane_copies(kb_v, s_v, k3s, k3r)
    q1 = plane_copies(qs_v, qr_v, q1s, q1r)
    q2 = z_copies(qt_v, qz_v, q2s, q2r)
    q3 = plane_copies(qb_v, t_v, q3s, q3r)

    def slice_of(colour, q):
        axis = COLOURS[colour][1]
        if axis == 0:
            return gt_v.at[q, pl.ds(2 * half, 2)]
        if axis == 1:
            return gt_v.at[pl.ds(2 * half, 2), q]
        return gt_v.at[pl.ds(2 * half, 2), :, q]

    def g_copy(colour, d):
        axis = COLOURS[colour][1]
        return remote(
            slice_of(colour, (pos[axis] + d) % SIDE),
            gb_v.at[colour, d, pl.ds(2 * half, 2)],
            gs.at[colour, d], gr.at[colour, d], axis_peer(axis, d),
        )

    def g_pass(colour, d):
        part = gb_v.at[colour, d, pl.ds(2 * half, 2)]
        return remote(part, part, fs.at[colour, d], fr.at[colour, d], partner)

    def a_copy(unit, d):
        colour, lo, hi = UNITS[unit]
        axis = COLOURS[colour][1]
        return remote(
            ab_v.at[0, :, lo:hi], ab_v.at[d, :, lo:hi],
            as_.at[unit, d], ar.at[unit, d], axis_peer(axis, d),
        )

    def s2_copy(unit, d):
        colour, lo, hi = UNITS[unit]
        axis = COLOURS[colour][2]
        return remote(
            s2_v.at[(pos[axis] + d) % SIDE, :, lo:hi], r2_v.at[d, :, lo:hi],
            b2s.at[unit, d], b2r.at[unit, d], axis_peer(axis, d),
        )

    def s3_copy(unit, d):
        colour, lo, hi = UNITS[unit]
        axis = COLOURS[colour][3]
        return remote(
            s3_v.at[(pos[axis] + d) % SIDE, :, lo:hi], r3_v.at[d, :, lo:hi],
            b3s.at[unit, d], b3r.at[unit, d], axis_peer(axis, d),
        )

    def product(unit):
        colour, lo, hi = UNITS[unit]
        axis = COLOURS[colour][2]
        if unit < 3:
            for d in (1, 3, 2):
                g_pass(colour, d).wait_recv()
        for d in (1, 3, 2):
            a_copy(unit, d).wait_recv()
        for o in range(SIDE):
            value = dot(gb_v[colour, 0, o].reshape(128, ROWS), ab_v[0, :, lo:hi])
            for d in (1, 2, 3):
                value = value + dot(gb_v[colour, d, o].reshape(128, ROWS), ab_v[d, :, lo:hi])
            value = value.astype(BF16)
            if axis == 2:
                for i in range(SIDE):
                    s2_v[i, o * BLOCK:(o + 1) * BLOCK, lo:hi] = value[i * BLOCK:(i + 1) * BLOCK]
            else:
                s2_v[o, :, lo:hi] = value
        for d in (1, 3, 2):
            s2_copy(unit, d).start()

    def own_slices():
        gb_v[0, 0] = gt_v[z]
        gb_v[1, 0] = gt_v[:, x]
        gb_v[2, 0] = gt_v[:, :, y]

    def pass_on(colour):
        for d in (1, 3, 2):
            g_copy(colour, d).wait_recv()
            g_pass(colour, d).start()

    def send_g(colour):
        for d in (1, 3, 2):
            g_copy(colour, d).start()

    load_k.wait()
    load_v.wait()
    summarise(k_v, v_v, ks_v, last)
    kr_v[me] = ks_v[me]
    load_q.wait()
    lax.fori_loop(0, HEADS, attend_head, 0, unroll=True)
    load_g.wait()
    flip(half)
    pl.semaphore_wait(barrier, PLANE - 1 + 3 + 1)

    start_all(k1, PLANE)
    give_g.start()
    send_g(1)
    send_g(2)
    give_g.wait_recv()
    load_w.wait()
    lax.fori_loop(0, WIDTH // 256, grad_chunk, 0, unroll=True)
    summarise(q_v, gh_v, qs_v, first)
    qr_v[me] = qs_v[me]
    flip(1 - half)
    recv_all(k1, PLANE)
    scan_plane(kr_v, kp_v, kt_v, False)
    start_all(k2, SIDE)
    send_g(0)
    own_slices()
    recv_all(k2, SIDE)
    finish_prefix(kr_v, kp_v, kz_v, kb_v, False, k3)
    s_v[me] = kb_v[me]
    start_all(q1, PLANE)
    lax.fori_loop(0, HEADS, pulled_head, 0, unroll=True)

    recv_all(k3, PLANE)
    for unit, (_, lo, hi) in enumerate(UNITS):
        lax.fori_loop(lo // HD, hi // HD, out_head, 0, unroll=True)
        for d in (1, 3, 2):
            a_copy(unit, d).start()
    pass_on(1)
    pass_on(2)
    pass_on(0)
    recv_all(q1, PLANE)
    scan_plane(qr_v, qp_v, qt_v, True)
    start_all(q2, SIDE)
    lax.fori_loop(0, HEADS, dq_head, 0, unroll=True)
    put_q = pltpu.make_async_copy(q_v, dq_hbm, loc.at[5])
    put_q.start()
    for unit in range(3):
        product(unit)
    recv_all(q2, SIDE)
    finish_prefix(qr_v, qp_v, qz_v, qb_v, True)
    t_v[me] = qb_v[me]
    start_all(q3, PLANE)
    for unit in range(3, len(UNITS)):
        product(unit)
    for unit, (colour, lo, hi) in enumerate(UNITS):
        axis = COLOURS[colour][2]
        for d in (1, 3, 2):
            s2_copy(unit, d).wait_recv()
        for i in range(SIDE):
            rows = slice(i * BLOCK, (i + 1) * BLOCK)
            value = s2_v[pos[axis], rows, lo:hi].astype(F32)
            for d in (1, 2, 3):
                value = value + r2_v[d, rows, lo:hi].astype(F32)
            s3_v[i, :, lo:hi] = value.astype(BF16)
        for d in (1, 3, 2):
            s3_copy(unit, d).start()
    recv_all(q3, PLANE)
    lax.fori_loop(0, HEADS, kv_head, 0, unroll=True)
    put_k = pltpu.make_async_copy(k_v, dk_hbm, loc.at[6])
    put_v = pltpu.make_async_copy(v_v, dv_hbm, loc.at[7])
    put_k.start()
    put_v.start()
    for unit, (colour, lo, hi) in enumerate(UNITS):
        axis = COLOURS[colour][3]
        for d in (1, 3, 2):
            s3_copy(unit, d).wait_recv()
        value = s3_v[pos[axis], :, lo:hi].astype(F32)
        for d in (1, 2, 3):
            value = value + r3_v[d, :, lo:hi].astype(F32)
        value = value * weight_factor
        for h in range(lo // HD, hi // HD):
            gw_v[:, h, :] = value[:, h * HD - lo:(h + 1) * HD - lo]
    put_w = pltpu.make_async_copy(gw_v, gw_hbm, loc.at[8])
    put_w.start()

    give_g.wait_send()
    for make in (k1, q1, k3, q3):
        sent_all(make, PLANE)
    for make in (k2, q2):
        sent_all(make, SIDE)
    for colour in range(3):
        for d in (1, 2, 3):
            g_copy(colour, d).wait_send()
            g_pass(colour, d).wait_send()
    for unit in range(len(UNITS)):
        for d in (1, 2, 3):
            a_copy(unit, d).wait_send()
            s2_copy(unit, d).wait_send()
            s3_copy(unit, d).wait_send()
    for put in (put_q, put_k, put_v, put_w):
        put.wait()


def put_out(a, b, c, e, oa, ob, oc, oe, va, vb, vc, ve, into, out):
    gets = [
        pltpu.make_async_copy(s, v, into.at[i])
        for i, (s, v) in enumerate(((a, va), (b, vb), (c, vc), (e, ve)))
    ]
    puts = [
        pltpu.make_async_copy(v, o, out.at[i])
        for i, (v, o) in enumerate(((va, oa), (vb, ob), (vc, oc), (ve, oe)))
    ]
    for get in gets:
        get.start()
    for get, put in zip(gets, puts):
        get.wait()
        put.start()
    for put in puts:
        put.wait()


def local(queries, keys, values, out_weight, grad_out, doc_ids):
    total_rows = ROWS * lax.axis_size("ctx")
    factor = 1.0 / math.sqrt(HD * total_rows / DOCS)
    weight_factor = 1.0 / math.sqrt(total_rows)
    dma = pltpu.SemaphoreType.DMA

    def vm(*shape, dtype=BF16):
        return pltpu.VMEM(shape, dtype)

    prefix = [
        vm(PLANE, PIECE + 16, HD), vm(PLANE, PIECE + 16, HD), vm(PIECE + 16, HD),
        vm(SIDE, PIECE + 16, HD), vm(PLANE, PIECE, HD, dtype=F32), vm(PLANE, PIECE, HD),
        vm(PLANE, PIECE, HD),
    ]
    prefix_sems = [dma((PLANE,)), dma((PLANE,)), dma((SIDE,)), dma((SIDE,)), dma((PLANE,)), dma((PLANE,))]
    flat = (ROWS, WIDTH)
    scratch = [
        vm(*flat), vm(*flat), vm(*flat), vm(WIDTH, MODEL), vm(2, *flat), vm(*flat),
        vm(SIDE, SIDE, SIDE, BLOCK, ROWS),
        vm(ROWS, HD, dtype=F32), vm(ROWS, ROWS, dtype=F32), vm(HEADS, ROWS, ROWS),
        vm(*flat, dtype=F32), vm(*flat, dtype=F32), vm(*flat, dtype=F32),
        vm(*flat, dtype=F32), vm(BLOCK, HEADS, HD, dtype=F32),
        *prefix, *prefix,
        vm(3, SIDE, SIDE, SIDE, BLOCK, ROWS), vm(SIDE, *flat),
        vm(SIDE, 128, WIDTH), vm(SIDE, 128, WIDTH), vm(SIDE, BLOCK, WIDTH), vm(SIDE, BLOCK, WIDTH),
        dma((9,)), dma(()), dma(()),
        *prefix_sems, *prefix_sems,
        *[dma((3, SIDE)) for _ in range(4)],
        *[dma((len(UNITS), SIDE)) for _ in range(6)],
    ]
    any_space = pl.BlockSpec(memory_space=pl.ANY)
    shape = jax.ShapeDtypeStruct
    outs = (
        shape(flat, BF16), shape(flat, BF16), shape(flat, BF16), shape((BLOCK, HEADS, HD), F32),
    )
    results = pl.pallas_call(
        lambda *refs: kernel(factor, weight_factor, *refs),
        out_shape=outs,
        in_specs=[pl.BlockSpec(memory_space=pltpu.VMEM)] + [any_space] * 5,
        out_specs=(any_space,) * 4,
        scratch_shapes=scratch,
        compiler_params=pltpu.CompilerParams(collective_id=0, has_side_effects=True),
        name="linear_attention_backward",
    )(doc_ids.reshape(1, ROWS), queries, keys, values, out_weight, grad_out)
    return pl.pallas_call(
        put_out,
        out_shape=outs,
        in_specs=[any_space] * 4,
        out_specs=(any_space,) * 4,
        scratch_shapes=[
            vm(*flat), vm(*flat), vm(*flat), vm(BLOCK, HEADS, HD, dtype=F32), dma((4,)), dma((4,)),
        ],
        name="results",
    )(*results)


def solution(mesh):
    return jax.shard_map(
        local,
        mesh=mesh,
        in_specs=(
            P("ctx", "head"),
            P("ctx", "head"),
            P("ctx", "head"),
            P("head", None),
            P("ctx", "head"),
            P("ctx"),
        ),
        out_specs=(P("ctx", "head"), P("ctx", "head"), P("ctx", "head"), P("ctx", "head", None)),
        check_vma=False,
    )
```
